32 devices in a mesh: parts: 2 (over x), chan: 4 (over y, core), tmpl: 4 (over z).
Axes of the slice: x: 2, y: 2, z: 4, core: 2. Of those that a mesh axis runs over, the one named last changes fastest.
Arguments:
- raw_traces: float32 [4096, 2816], P(('chan', 'tmpl'), 'parts'), parts along dimension 1, may hold values from -50 to 50
- filter_taps: float32 [129], replicated, may hold values from -0.5 to 0.5
- templates: bfloat16 [32, 200, 4096], P('tmpl', None, 'chan'), may hold values from -6 to 6
- offsets: int32 [32], P('tmpl'), may hold values from 0 to 56
- channel_mask: int32 [32, 4096], P('tmpl'), may hold values from 0 to 1, as said below
Outputs:
- detection: float32 [32, 2048], P('tmpl', ('parts', 'chan')), parts along dimension 1
The draws below stay inside these ranges and needn't reach their ends.
There are 2 independent parts, one for each index of `parts`. The reference program is written for one: setup_inputs(seed, part) draws one part's arguments, and reference() takes and returns one part's arrays. A program takes and returns all parts, laid end to end along the dimension named above; an argument that names none is the same for every part. Nothing has to cross between parts.
Inputs may be any that keep to these rules, and one draw needn't show every extreme that they name: `channel_mask`: each template uses one contiguous run of 4 or more blocks of 128 channels, starting and ending at multiples of 128; some template uses all channels.
All inputs are finite; a program needn't handle non-finite values.
Results may differ from the reference program's by a relative error of at most 0.004.
Values may be sent and summed in bfloat16 or wider, within the bound.
A program may use at most 128 MiB of HBM per device.

```python
import math
import jax
import jax.numpy as jnp
from jax import lax

CHANNELS = 4096
TMPL_LEN = 200
SPAN = 256
FIR_TAPS = 129
TEMPLATES = 32
LAGS = 1024
SAMPLES = 1408


def draw_raw_traces(key, part):
    key_gain, key_noise = jax.random.split(key, 2)
    gains = jnp.exp(jax.random.uniform(key_gain, (CHANNELS, 1), jnp.float32, 0.0, math.log(10.0)))
    noise = jnp.clip(jax.random.normal(key_noise, (CHANNELS, SAMPLES), jnp.float32), -5.0, 5.0)
    return (gains * noise).astype(jnp.float32)


def draw_channel_mask(key, part):
    key_span, key_first, key_full = jax.random.split(jax.random.fold_in(key, 7), 3)
    unit_width = CHANNELS // 32
    span_units = jax.random.randint(key_span, (TEMPLATES, 1), 4, 33)
    full_row = jax.random.randint(key_full, (), 0, TEMPLATES)
    rows_index = jnp.arange(TEMPLATES, dtype=jnp.int32)[:, None]
    span_units = jnp.where(rows_index == full_row, 32, span_units)
    first_unit = jax.random.randint(key_first, (TEMPLATES, 1), 0, 33 - span_units)
    columns = jnp.arange(CHANNELS, dtype=jnp.int32)[None, :] // unit_width
    inside = (columns >= first_unit) & (columns < first_unit + span_units)
    return inside.astype(jnp.int32)


def with_ends(entries, rng, least, largest):
    dims = entries.shape
    place = [jax.random.randint(jax.random.fold_in(rng, axis), (), 0, dims[axis]) for axis in range(len(dims))]
    entries = entries.at[tuple(place)].set(least)
    longest = dims.index(max(dims))
    place[longest] = (place[longest] + 1) % dims[longest]
    return entries.at[tuple(place)].set(largest)


def block_scale(stream_key, extent, shards, smallest, top_value):
    level = 1.0
    for position, blocks in shards:
        heights = jax.random.uniform(jax.random.fold_in(jax.random.fold_in(stream_key, 6), position), (blocks,), jnp.float32, smallest / len(shards), top_value / len(shards))
        level = level * jnp.repeat(jnp.exp(heights), extent[position] // blocks).reshape((-1,) + (1,) * (len(extent) - 1 - position))
    return level


def bell_draw(rng, extent, width, reach, shards=(), held_as=jnp.bfloat16):
    entries = jax.random.normal(rng, extent, jnp.float32) * width
    if len(shards) > 0:
        entries = block_scale(rng, extent, shards, -0.22, 0.18) * entries
    return jnp.clip(entries, min=-reach, max=reach).astype(held_as)


def setup_inputs(seed: int = 0, part: int = 0) -> dict:
    streams_of = jax.random.split(jax.random.key(seed), 6)
    part_keys = jax.random.split(jax.random.fold_in(streams_of[5], part), 6)
    return {
        "raw_traces": draw_raw_traces(jax.random.fold_in(jax.random.fold_in(streams_of[5], part), 71), part),
        "filter_taps": bell_draw(streams_of[1], (FIR_TAPS,), FIR_TAPS ** -0.5, 0.5, (), jnp.float32),
        "templates": bell_draw(streams_of[2], (TEMPLATES, TMPL_LEN, CHANNELS), 1.0, 6.0, ((0, 4), (2, 4))),
        "offsets": with_ends(jax.random.randint(streams_of[3], (TEMPLATES,), 0, SPAN - TMPL_LEN + 1), jax.random.fold_in(streams_of[3], 1), 0, SPAN - TMPL_LEN).astype(jnp.int32),
        "channel_mask": draw_channel_mask(jax.random.fold_in(streams_of[5], 71), part),
    }


def filter_traces(raw_traces, filter_taps):
    output = lax.conv_general_dilated(raw_traces[:, None, :], filter_taps[None, None, :], (1,), 'VALID', precision=lax.Precision.HIGHEST)
    return lax.optimization_barrier(output[:, 0, :].astype(jnp.bfloat16))

def shape_templates(templates, channel_mask):
    values = templates.astype(jnp.float32)
    rms_scale = jnp.sqrt(lax.optimization_barrier(jnp.mean(values * values, axis=1, keepdims=True)) + 1e-06)
    return (channel_mask.astype(jnp.float32)[:, None, :] * values / rms_scale).astype(jnp.bfloat16)

def skew_sum(product, count_out):
    height, length = product.shape
    flattened = jnp.concatenate([product.reshape(-1), jnp.zeros((height,), product.dtype)])
    return flattened.reshape(height, length + 1)[:, :count_out].sum(axis=0)

def window_energy(masses, offsets, count_out):

    def one_row(row_values, offset_value):
        return lax.dynamic_slice_in_dim(row_values, offset_value, count_out + TMPL_LEN - 1)
    segments = jax.vmap(one_row)(masses, offsets)
    return lax.reduce_window(segments, jnp.zeros((), segments.dtype), lax.add, (1, TMPL_LEN), (1, 1), 'VALID')

def reference(raw_traces, filter_taps, templates, offsets, channel_mask):
    filtered = filter_traces(raw_traces, filter_taps)
    shaped = shape_templates(templates, channel_mask)

    def one_template(inputs):
        weights, offset_value = inputs
        window = lax.dynamic_slice_in_dim(filtered, offset_value, LAGS + TMPL_LEN - 1, 1)
        product = jnp.dot(weights, window, preferred_element_type=jnp.float32)
        return skew_sum(product, LAGS)
    numerator = lax.map(one_template, (shaped, offsets))
    squares = filtered.astype(jnp.float32) ** 2
    masses = jnp.dot(channel_mask.astype(jnp.float32), squares, precision=lax.Precision.HIGHEST)
    energy = window_energy(masses, offsets, LAGS)
    return numerator / jnp.sqrt(energy)
```

```python
import functools

import jax
import jax.numpy as jnp
from jax import lax
from jax.experimental import pallas as pl
from jax.experimental.pallas import tpu as pltpu
from jax.sharding import PartitionSpec as P

SPAN = 256
BLK = 256
LANE = 128
MESH = pl.DeviceIdType.MESH


def left(x, count):
    size = x.shape[-1]
    count = count % size
    return x if count == 0 else pltpu.roll(x, size - count, x.ndim - 1)


def kernel(
    ntm, nch, raw_hbm, taps_ref, tmpl_hbm, mask_hbm, offs_ref, out_ref,
    raw, tap_row, tmpl, mask, skewed, shaped, rall, prod, qacc, units, num_out, en_out,
    num_in, en_in, load_sem, recv_sem, right_sem, left_sem, unit_send, unit_recv,
    num_send, num_recv, en_send, en_recv,
):
    z = lax.axis_index("tmpl")
    c = lax.axis_index("chan")
    rows = raw.shape[0]
    group, tlen, local = tmpl.shape
    nblk = rall.shape[0]
    total = nblk * BLK
    unit = min(LANE, rows)
    nun = rows // unit

    loads = [
        pltpu.make_async_copy(raw_hbm, raw, load_sem.at[0]),
        pltpu.make_async_copy(tmpl_hbm, tmpl, load_sem.at[1]),
        pltpu.make_async_copy(
            mask_hbm.at[:, pl.ds(pl.multiple_of(c * local, LANE), local)], mask, load_sem.at[2]
        ),
    ]
    for item in loads:
        item.start()

    barrier = pltpu.get_barrier_semaphore()
    for d in range(1, ntm):
        pl.semaphore_signal(
            barrier, inc=1, device_id={"tmpl": lax.rem(z + d, ntm)}, device_id_type=MESH
        )
    for d in range(1, nch):
        pl.semaphore_signal(
            barrier, inc=1, device_id={"chan": lax.rem(c + d, nch)}, device_id_type=MESH
        )

    tap_row[...] = jnp.zeros_like(tap_row)
    tap_row[:, : taps_ref.shape[1]] = taps_ref[...]
    band = pltpu.roll(
        jnp.broadcast_to(tap_row[...], (LANE, 2 * LANE)), 0, 1, stride=1, stride_axis=0
    )
    band_hi = band.astype(jnp.bfloat16)
    band_lo = (band - band_hi.astype(jnp.float32)).astype(jnp.bfloat16)
    qacc[...] = jnp.zeros_like(qacc)
    loads[0].wait()
    pl.semaphore_wait(barrier, ntm - 1 + nch - 1)

    def chunk(src, n):
        return rall.at[n, pl.ds(pl.multiple_of(src * rows, rows), rows), :]

    def hop(src, n, sems, step):
        return pltpu.make_async_remote_copy(
            src_ref=chunk(src, n),
            dst_ref=chunk(src, n),
            send_sem=sems.at[src, n],
            recv_sem=recv_sem.at[src, n],
            device_id={"tmpl": lax.rem(z + step + ntm, ntm)},
            device_id_type=MESH,
        )

    def contract(a, b):
        return lax.dot_general(
            a, b, (((1,), (1,)), ((), ())), preferred_element_type=jnp.float32
        )

    def fir(n, carry):
        x = raw[:, pl.ds(pl.multiple_of(n * BLK, BLK), BLK + LANE)]
        hi = x.astype(jnp.bfloat16)
        lo = (x - hi.astype(jnp.float32)).astype(jnp.bfloat16)
        for half in range(BLK // LANE):
            a = hi[:, half * LANE : half * LANE + 2 * LANE]
            b = lo[:, half * LANE : half * LANE + 2 * LANE]
            y = contract(a, band_hi) + (contract(b, band_hi) + contract(a, band_lo))
            y = y.astype(jnp.bfloat16)
            rall[
                n, pl.ds(pl.multiple_of(z * rows, rows), rows), half * LANE : half * LANE + LANE
            ] = y
            y = y.astype(jnp.float32)
            y = y * y
            at = pl.ds(pl.multiple_of(n * BLK + half * LANE, LANE), LANE)
            for u in range(nun):
                units[z, u : u + 1, at] = jnp.sum(
                    y[u * unit : (u + 1) * unit], axis=0, keepdims=True
                )

        @pl.when(z < ntm - 1)
        def _():
            hop(z, n, right_sem, 1).start()

        @pl.when(z > 0)
        def _():
            hop(z, n, left_sem, -1).start()

        return carry

    lax.fori_loop(0, nblk, fir, 0)

    def unit_copy(src, d):
        return pltpu.make_async_remote_copy(
            src_ref=units.at[src],
            dst_ref=units.at[src],
            send_sem=unit_send.at[d],
            recv_sem=unit_recv.at[d],
            device_id={"tmpl": lax.rem(z + d, ntm)},
            device_id_type=MESH,
        )

    for d in range(1, ntm):
        unit_copy(z, d).start()

    loads[1].wait()
    loads[2].wait()

    def shape_cols(i, carry):
        cols = pl.ds(pl.multiple_of(i * LANE, LANE), LANE)
        flags = mask[:, cols].astype(jnp.float32)
        for k in range(group):
            v = tmpl[k, :, cols].astype(jnp.float32)
            power = jnp.mean(v * v, axis=0, keepdims=True)
            scale = flags[k : k + 1, :] / jnp.sqrt(power + 1e-06)
            skewed[pl.ds(k, tlen, stride=group), :] = v * scale
        shaped[:, cols] = skewed[...].astype(jnp.bfloat16)
        return carry

    lax.fori_loop(0, local // LANE, shape_cols, 0)

    offs = jnp.zeros((group, 1), jnp.int32)
    index = lax.broadcasted_iota(jnp.int32, (group, 1), 0)
    for k in range(group):
        offs = jnp.where(index == k, offs_ref[k], offs)

    def shift_rows(x):
        amount = jnp.broadcast_to(offs, x.shape)
        bit = 1
        while bit < SPAN - tlen + 1:
            x = jnp.where((amount & bit) != 0, left(x, bit), x)
            bit *= 2
        return x

    def spread(x, own_ref, in_ref, send, recv):
        lag = own_ref.shape[2]
        for j in range(nch):
            own_ref[j] = x[:, j * lag : (j + 1) * lag]
        for d in range(1, nch):
            other = lax.rem(c + d, nch)
            pltpu.make_async_remote_copy(
                src_ref=own_ref.at[other],
                dst_ref=in_ref.at[d],
                send_sem=send.at[d],
                recv_sem=recv.at[d],
                device_id={"chan": other},
                device_id_type=MESH,
            ).start()

    def collect(own_ref, in_ref, send, recv):
        value = own_ref[c]
        for d in range(1, nch):
            pltpu.make_async_remote_copy(
                src_ref=own_ref.at[lax.rem(c + d, nch)],
                dst_ref=in_ref.at[d],
                send_sem=send.at[d],
                recv_sem=recv.at[d],
                device_id={"chan": lax.rem(c + d, nch)},
                device_id_type=MESH,
            ).wait()
            value = value + in_ref[d]
        return value

    for d in range(1, ntm):
        unit_copy(lax.rem(z + ntm - d, ntm), d).wait()
    masses = jnp.zeros((group, total), jnp.float32)
    for s in range(ntm):
        for u in range(nun):
            at = s * rows + u * unit
            flag = mask[:, at : at + 1].astype(jnp.float32)
            masses = masses + flag * units[s, u : u + 1, :]
    window, width, place, energy = masses, 1, 0, None
    while width <= tlen:
        if tlen & width:
            piece = left(window, place)
            energy = piece if energy is None else energy + piece
            place += width
        window = window + left(window, width)
        width *= 2
    spread(shift_rows(energy), en_out, en_in, en_send, en_recv)

    def arrive(d, n):
        @pl.when(z - d >= 0)
        def _():
            src = lax.rem(z - d + ntm, ntm)
            hop(src, n, right_sem, 1).wait_recv()

            @pl.when(z < ntm - 1)
            def _():
                hop(src, n, right_sem, 1).start()

        @pl.when(z + d < ntm)
        def _():
            src = lax.rem(z + d, ntm)
            hop(src, n, left_sem, -1).wait_recv()

            @pl.when(z > 0)
            def _():
                hop(src, n, left_sem, -1).start()

    def block(n, carry):
        arrive(ntm - 1, n)
        prod[...] = jnp.dot(shaped[...], rall[n], preferred_element_type=jnp.float32)
        blank = jnp.zeros((group, LANE), jnp.float32)
        total_acc = jnp.zeros((group, 2 * BLK), jnp.float32)
        for g in range(min(LANE, tlen)):
            low = prod[group * g : group * (g + 1), :]
            first, second = low[:, :LANE], low[:, LANE:]
            carry_in = blank
            if g + LANE < tlen:
                high = prod[group * (g + LANE) : group * (g + LANE + 1), :]
                carry_in = high[:, :LANE]
                first = first + high[:, LANE:]
            wide = jnp.concatenate([blank, carry_in, first, second], axis=1)
            total_acc = total_acc + left(wide, g)
        at = pl.ds(pl.multiple_of(n * BLK, BLK), 2 * BLK)
        qacc[:, at] = qacc[:, at] + total_acc
        return carry

    def step(d):
        def body(n, carry):
            arrive(d, n)
            return carry

        lax.fori_loop(0, nblk, body, 0)

    for d in range(1, ntm - 1):
        step(d)
    lax.fori_loop(0, nblk, block, 0)

    spread(shift_rows(qacc[:, BLK:]), num_out, num_in, num_send, num_recv)
    energy = collect(en_out, en_in, en_send, en_recv)
    numerator = collect(num_out, num_in, num_send, num_recv)
    out_ref[...] = numerator / jnp.sqrt(energy)

    def drain(n, carry):
        for s in range(ntm):
            @pl.when((s <= z) & (z < ntm - 1))
            def _():
                hop(s, n, right_sem, 1).wait_send()

            @pl.when((s >= z) & (z > 0))
            def _():
                hop(s, n, left_sem, -1).wait_send()

        return carry

    lax.fori_loop(0, nblk, drain, 0)


def shards(raw_traces, filter_taps, templates, offsets, channel_mask):
    ntm = lax.axis_size("tmpl")
    nch = lax.axis_size("chan")
    rows, length = raw_traces.shape
    group, tlen, local = templates.shape
    nblk = (length - filter_taps.shape[0] + 1) // BLK
    total = nblk * BLK
    lag = (total - SPAN) // nch
    nun = rows // min(LANE, rows)
    f32, bf16, dma = jnp.float32, jnp.bfloat16, pltpu.SemaphoreType.DMA
    any_spec = pl.BlockSpec(memory_space=pl.ANY)
    vmem_spec = pl.BlockSpec(memory_space=pltpu.VMEM)
    return pl.pallas_call(
        functools.partial(kernel, ntm, nch),
        out_shape=jax.ShapeDtypeStruct((group, lag), f32),
        in_specs=[
            any_spec, vmem_spec, any_spec, any_spec, pl.BlockSpec(memory_space=pltpu.SMEM),
        ],
        out_specs=vmem_spec,
        scratch_shapes=[
            pltpu.VMEM((rows, length), f32),
            pltpu.VMEM((1, 2 * LANE), f32),
            pltpu.VMEM((group, tlen, local), bf16),
            pltpu.VMEM((group, local), jnp.int32),
            pltpu.VMEM((group * tlen, LANE), f32),
            pltpu.VMEM((group * tlen, local), bf16),
            pltpu.VMEM((nblk, local, BLK), bf16),
            pltpu.VMEM((group * tlen, BLK), f32),
            pltpu.VMEM((group, BLK + total), f32),
            pltpu.VMEM((ntm, nun, total), f32),
            pltpu.VMEM((nch, group, lag), f32),
            pltpu.VMEM((nch, group, lag), f32),
            pltpu.VMEM((nch, group, lag), f32),
            pltpu.VMEM((nch, group, lag), f32),
            dma((3,)),
            dma((ntm, nblk)),
            dma((ntm, nblk)),
            dma((ntm, nblk)),
            dma((ntm,)),
            dma((ntm,)),
            dma((nch,)),
            dma((nch,)),
            dma((nch,)),
            dma((nch,)),
        ],
        compiler_params=pltpu.CompilerParams(
            collective_id=0, has_side_effects=True, vmem_limit_bytes=48 * 1024 * 1024
        ),
    )(raw_traces, filter_taps.reshape(1, -1), templates, channel_mask, offsets)


def solution(mesh):
    placed = (
        P(("chan", "tmpl"), "parts"),
        P(),
        P("tmpl", None, "chan"),
        P("tmpl"),
        P("tmpl", None),
    )
    return jax.shard_map(
        shards, mesh=mesh, in_specs=placed, out_specs=P("tmpl", ("parts", "chan")), check_vma=False
    )
```

```python
import functools

import jax
import jax.numpy as jnp
from jax import lax
from jax.experimental import pallas as pl
from jax.experimental.pallas import tpu as pltpu
from jax.sharding import PartitionSpec as P

SPAN = 256
BLK = 256
LANE = 128
MESH = pl.DeviceIdType.MESH


def left(x, count):
    size = x.shape[-1]
    count = count % size
    return x if count == 0 else pltpu.roll(x, size - count, x.ndim - 1)


def kernel(
    ntm, nch, lend, raw_hbm, taps_ref, tmpl_hbm, mask_hbm, offs_ref, out_ref,
    raw, tap_row, tmpl, mask, skewed, shaped, rall, prod, qacc, units, num_out, en_out,
    num_in, en_in, guest, gacc, gsum, load_sem, raw_sem, recv_sem, right_sem, left_sem,
    unit_right, unit_left, unit_recv, num_send, num_recv, en_send, en_recv, guest_sem, gsum_sem,
):
    z = lax.axis_index("tmpl")
    c = lax.axis_index("chan")
    rows = raw.shape[0]
    group, tlen, local = tmpl.shape
    nblk = rall.shape[0]
    total = nblk * BLK
    unit = min(LANE, rows)
    nun = rows // unit

    def load_raw(n, first):
        at = pl.ds(0, BLK + LANE) if first else pl.ds(pl.multiple_of(n * BLK + LANE, LANE), BLK)
        return pltpu.make_async_copy(raw_hbm.at[:, at], raw.at[:, at], raw_sem.at[n])

    for n in range(nblk):
        load_raw(n, n == 0).start()
    loads = [
        pltpu.make_async_copy(tmpl_hbm, tmpl, load_sem.at[0]),
        pltpu.make_async_copy(
            mask_hbm.at[:, pl.ds(pl.multiple_of(c * local, LANE), local)], mask, load_sem.at[1]
        ),
    ]
    for item in loads:
        item.start()

    barrier = pltpu.get_barrier_semaphore()
    @pl.when(z < ntm - 1)
    def _():
        pl.semaphore_signal(
            barrier, inc=1, device_id={"tmpl": lax.rem(z + 1, ntm)}, device_id_type=MESH
        )

    @pl.when(z > 0)
    def _():
        pl.semaphore_signal(
            barrier, inc=1, device_id={"tmpl": lax.rem(z - 1 + ntm, ntm)}, device_id_type=MESH
        )

    for d in range(1, nch):
        pl.semaphore_signal(
            barrier, inc=1, device_id={"chan": lax.rem(c + d, nch)}, device_id_type=MESH
        )

    tap_row[...] = jnp.zeros_like(tap_row)
    tap_row[:, : taps_ref.shape[1]] = taps_ref[...]
    band = pltpu.roll(
        jnp.broadcast_to(tap_row[...], (LANE, 2 * LANE)), 0, 1, stride=1, stride_axis=0
    )
    band_hi = band.astype(jnp.bfloat16)
    band_lo = (band - band_hi.astype(jnp.float32)).astype(jnp.bfloat16)
    qacc[...] = jnp.zeros_like(qacc)
    is_end = (z == 0) | (z == ntm - 1)
    is_helper = (z == 1) | (z == ntm - 2)
    inward = jnp.where(z == 0, 1, ntm - 2)
    outward = jnp.where(z == 1, 0, ntm - 1)
    if lend:
        @pl.when(is_end)
        def _():
            at = pl.ds(pl.multiple_of(inward * rows, rows), rows)
            for n in range(nblk):
                rall[n, at, :] = jnp.zeros((rows, BLK), jnp.bfloat16)

    load_raw(0, True).wait()
    pl.semaphore_wait(
        barrier, jnp.where(z < ntm - 1, 1, 0) + jnp.where(z > 0, 1, 0) + (nch - 1)
    )

    def chunk(src, n):
        return rall.at[n, pl.ds(pl.multiple_of(src * rows, rows), rows), :]

    def hop(src, n, sems, step):
        return pltpu.make_async_remote_copy(
            src_ref=chunk(src, n),
            dst_ref=chunk(src, n),
            send_sem=sems.at[src, n],
            recv_sem=recv_sem.at[src, n],
            device_id={"tmpl": lax.rem(z + step + ntm, ntm)},
            device_id_type=MESH,
        )

    def contract(a, b):
        return lax.dot_general(
            a, b, (((1,), (1,)), ((), ())), preferred_element_type=jnp.float32
        )

    def fir(n, carry):
        x = raw[:, pl.ds(pl.multiple_of(n * BLK, BLK), BLK + LANE)]
        hi = x.astype(jnp.bfloat16)
        lo = (x - hi.astype(jnp.float32)).astype(jnp.bfloat16)
        for half in range(BLK // LANE):
            a = hi[:, half * LANE : half * LANE + 2 * LANE]
            b = lo[:, half * LANE : half * LANE + 2 * LANE]
            y = contract(a, band_hi) + (contract(b, band_hi) + contract(a, band_lo))
            y = y.astype(jnp.bfloat16)
            rall[
                n, pl.ds(pl.multiple_of(z * rows, rows), rows), half * LANE : half * LANE + LANE
            ] = y
            y = y.astype(jnp.float32)
            y = y * y
            at = pl.ds(pl.multiple_of(n * BLK + half * LANE, LANE), LANE)
            for u in range(nun):
                units[z, u : u + 1, at] = jnp.sum(
                    y[u * unit : (u + 1) * unit], axis=0, keepdims=True
                )

        @pl.when(z < ntm - 1 - lend)
        def _():
            hop(z, n, right_sem, 1).start()

        @pl.when(z > lend)
        def _():
            hop(z, n, left_sem, -1).start()

        return carry

    fir(0, 0)

    def fir_next(n, carry):
        load_raw(n, False).wait()
        return fir(n, carry)

    lax.fori_loop(1, nblk, fir_next, 0)

    def unit_hop(src, sems, step):
        return pltpu.make_async_remote_copy(
            src_ref=units.at[src],
            dst_ref=units.at[src],
            send_sem=sems.at[src],
            recv_sem=unit_recv.at[src],
            device_id={"tmpl": lax.rem(z + step + ntm, ntm)},
            device_id_type=MESH,
        )

    @pl.when(z < ntm - 1)
    def _():
        unit_hop(z, unit_right, 1).start()

    @pl.when(z > 0)
    def _():
        unit_hop(z, unit_left, -1).start()

    loads[0].wait()
    loads[1].wait()

    def shape_cols(i, carry):
        cols = pl.ds(pl.multiple_of(i * LANE, LANE), LANE)
        flags = mask[:, cols].astype(jnp.float32)
        for k in range(group):
            v = tmpl[k, :, cols].astype(jnp.float32)
            power = jnp.mean(v * v, axis=0, keepdims=True)
            scale = flags[k : k + 1, :] / jnp.sqrt(power + 1e-06)
            skewed[pl.ds(k, tlen, stride=group), :] = v * scale
        shaped[:, cols] = skewed[...].astype(jnp.bfloat16)
        return carry

    lax.fori_loop(0, local // LANE, shape_cols, 0)

    def lend_copy(peer):
        cols = pl.ds(pl.multiple_of(inward * rows, rows), rows)
        return pltpu.make_async_remote_copy(
            src_ref=shaped.at[:, cols],
            dst_ref=guest,
            send_sem=guest_sem.at[0],
            recv_sem=guest_sem.at[1],
            device_id={"tmpl": peer},
            device_id_type=MESH,
        )

    def gsum_copy(peer):
        return pltpu.make_async_remote_copy(
            src_ref=gacc.at[:, pl.ds(BLK, total)],
            dst_ref=gsum,
            send_sem=gsum_sem.at[0],
            recv_sem=gsum_sem.at[1],
            device_id={"tmpl": peer},
            device_id_type=MESH,
        )

    if lend:
        @pl.when(is_end)
        def _():
            lend_copy(inward).start()

    offs = jnp.zeros((group, 1), jnp.int32)
    index = lax.broadcasted_iota(jnp.int32, (group, 1), 0)
    for k in range(group):
        offs = jnp.where(index == k, offs_ref[k], offs)

    def shift_rows(x):
        amount = jnp.broadcast_to(offs, x.shape)
        bit = 1
        while bit < SPAN - tlen + 1:
            x = jnp.where((amount & bit) != 0, left(x, bit), x)
            bit *= 2
        return x

    def spread(x, own_ref, in_ref, send, recv):
        lag = own_ref.shape[2]
        for j in range(nch):
            own_ref[j] = x[:, j * lag : (j + 1) * lag]
        for d in range(1, nch):
            other = lax.rem(c + d, nch)
            pltpu.make_async_remote_copy(
                src_ref=own_ref.at[other],
                dst_ref=in_ref.at[d],
                send_sem=send.at[d],
                recv_sem=recv.at[d],
                device_id={"chan": other},
                device_id_type=MESH,
            ).start()

    def collect(own_ref, in_ref, send, recv):
        value = own_ref[c]
        for d in range(1, nch):
            pltpu.make_async_remote_copy(
                src_ref=own_ref.at[lax.rem(c + d, nch)],
                dst_ref=in_ref.at[d],
                send_sem=send.at[d],
                recv_sem=recv.at[d],
                device_id={"chan": lax.rem(c + d, nch)},
                device_id_type=MESH,
            ).wait()
            value = value + in_ref[d]
        return value

    for d in range(1, ntm):
        @pl.when(z - d >= 0)
        def _():
            src = lax.rem(z - d + ntm, ntm)
            unit_hop(src, unit_right, 1).wait_recv()

            @pl.when(z < ntm - 1)
            def _():
                unit_hop(src, unit_right, 1).start()

        @pl.when(z + d < ntm)
        def _():
            src = lax.rem(z + d, ntm)
            unit_hop(src, unit_left, -1).wait_recv()

            @pl.when(z > 0)
            def _():
                unit_hop(src, unit_left, -1).start()

    masses = jnp.zeros((group, total), jnp.float32)
    for s in range(ntm):
        for u in range(nun):
            at = s * rows + u * unit
            flag = mask[:, at : at + 1].astype(jnp.float32)
            masses = masses + flag * units[s, u : u + 1, :]
    window, width, place, energy = masses, 1, 0, None
    while width <= tlen:
        if tlen & width:
            piece = left(window, place)
            energy = piece if energy is None else energy + piece
            place += width
        window = window + left(window, width)
        width *= 2
    spread(shift_rows(energy), en_out, en_in, en_send, en_recv)

    def arrive(d, n):
        near = lend if d == 1 else 0

        @pl.when((z - d >= 0) & (z < ntm - near))
        def _():
            src = lax.rem(z - d + ntm, ntm)
            hop(src, n, right_sem, 1).wait_recv()

            @pl.when(z < ntm - 1)
            def _():
                hop(src, n, right_sem, 1).start()

        @pl.when((z + d < ntm) & (z >= near))
        def _():
            src = lax.rem(z + d, ntm)
            hop(src, n, left_sem, -1).wait_recv()

            @pl.when(z > 0)
            def _():
                hop(src, n, left_sem, -1).start()

    def skew(n, weights, samples, acc):
        prod[...] = jnp.dot(weights, samples, preferred_element_type=jnp.float32)
        blank = jnp.zeros((group, LANE), jnp.float32)
        total_acc = jnp.zeros((group, 2 * BLK), jnp.float32)
        for g in range(min(LANE, tlen)):
            low = prod[group * g : group * (g + 1), :]
            first, second = low[:, :LANE], low[:, LANE:]
            carry_in = blank
            if g + LANE < tlen:
                high = prod[group * (g + LANE) : group * (g + LANE + 1), :]
                carry_in = high[:, :LANE]
                first = first + high[:, LANE:]
            wide = jnp.concatenate([blank, carry_in, first, second], axis=1)
            total_acc = total_acc + left(wide, g)
        at = pl.ds(pl.multiple_of(n * BLK, BLK), 2 * BLK)
        acc[:, at] = acc[:, at] + total_acc

    def block(n, carry):
        for d in range(max(1, ntm // 2), ntm):
            arrive(d, n)
        skew(n, shaped[...], rall[n], qacc)
        return carry

    def guest_block(n, carry):
        skew(n, guest[...], chunk(z, n)[...], gacc)
        return carry

    def step(d):
        def body(n, carry):
            arrive(d, n)
            return carry

        lax.fori_loop(0, nblk, body, 0)

    for d in range(1, max(1, ntm // 2)):
        step(d)
    lax.fori_loop(0, nblk, block, 0)

    if lend:
        @pl.when(is_helper)
        def _():
            gacc[...] = jnp.zeros_like(gacc)
            lend_copy(outward).wait_recv()
            lax.fori_loop(0, nblk, guest_block, 0)
            gsum_copy(outward).start()

        @pl.when(is_end)
        def _():
            gsum_copy(inward).wait_recv()
            qacc[:, BLK:] = qacc[:, BLK:] + gsum[...]

    spread(shift_rows(qacc[:, BLK:]), num_out, num_in, num_send, num_recv)
    energy = collect(en_out, en_in, en_send, en_recv)
    numerator = collect(num_out, num_in, num_send, num_recv)
    out_ref[...] = numerator / jnp.sqrt(energy)

    def drain(n, carry):
        for s in range(ntm):
            @pl.when((s <= z) & (z < ntm - 1) & ((s != z) | (z < ntm - 1 - lend)))
            def _():
                hop(s, n, right_sem, 1).wait_send()

            @pl.when((s >= z) & (z > 0) & ((s != z) | (z > lend)))
            def _():
                hop(s, n, left_sem, -1).wait_send()

        return carry

    lax.fori_loop(0, nblk, drain, 0)
    for s in range(ntm):
        @pl.when((s <= z) & (z < ntm - 1))
        def _():
            unit_hop(s, unit_right, 1).wait_send()

        @pl.when((s >= z) & (z > 0))
        def _():
            unit_hop(s, unit_left, -1).wait_send()

    if lend:
        @pl.when(is_end)
        def _():
            lend_copy(inward).wait_send()

        @pl.when(is_helper)
        def _():
            gsum_copy(outward).wait_send()


def shards(raw_traces, filter_taps, templates, offsets, channel_mask):
    ntm = lax.axis_size("tmpl")
    nch = lax.axis_size("chan")
    rows, length = raw_traces.shape
    group, tlen, local = templates.shape
    nblk = (length - filter_taps.shape[0] + 1) // BLK
    total = nblk * BLK
    lag = (total - SPAN) // nch
    nun = rows // min(LANE, rows)
    lend = int(ntm >= 4 and rows % LANE == 0)
    f32, bf16, dma = jnp.float32, jnp.bfloat16, pltpu.SemaphoreType.DMA
    any_spec = pl.BlockSpec(memory_space=pl.ANY)
    vmem_spec = pl.BlockSpec(memory_space=pltpu.VMEM)
    return pl.pallas_call(
        functools.partial(kernel, ntm, nch, lend),
        out_shape=jax.ShapeDtypeStruct((group, lag), f32),
        in_specs=[
            any_spec, vmem_spec, any_spec, any_spec, pl.BlockSpec(memory_space=pltpu.SMEM),
        ],
        out_specs=vmem_spec,
        scratch_shapes=[
            pltpu.VMEM((rows, length), f32),
            pltpu.VMEM((1, 2 * LANE), f32),
            pltpu.VMEM((group, tlen, local), bf16),
            pltpu.VMEM((group, local), jnp.int32),
            pltpu.VMEM((group * tlen, LANE), f32),
            pltpu.VMEM((group * tlen, local), bf16),
            pltpu.VMEM((nblk, local, BLK), bf16),
            pltpu.VMEM((group * tlen, BLK), f32),
            pltpu.VMEM((group, BLK + total), f32),
            pltpu.VMEM((ntm, nun, total), f32),
            pltpu.VMEM((nch, group, lag), f32),
            pltpu.VMEM((nch, group, lag), f32),
            pltpu.VMEM((nch, group, lag), f32),
            pltpu.VMEM((nch, group, lag), f32),
            pltpu.VMEM((group * tlen, rows if lend else LANE), bf16),
            pltpu.VMEM((group, BLK + total), f32),
            pltpu.VMEM((group, total), f32),
            dma((2,)),
            dma((nblk,)),
            dma((ntm, nblk)),
            dma((ntm, nblk)),
            dma((ntm, nblk)),
            dma((ntm,)),
            dma((ntm,)),
            dma((ntm,)),
            dma((nch,)),
            dma((nch,)),
            dma((nch,)),
            dma((nch,)),
            dma((2,)),
            dma((2,)),
        ],
        compiler_params=pltpu.CompilerParams(
            collective_id=0, has_side_effects=True, vmem_limit_bytes=60 * 1024 * 1024
        ),
    )(raw_traces, filter_taps.reshape(1, -1), templates, channel_mask, offsets)


def solution(mesh):
    placed = (
        P(("chan", "tmpl"), "parts"),
        P(),
        P("tmpl", None, "chan"),
        P("tmpl"),
        P("tmpl", None),
    )
    return jax.shard_map(
        shards, mesh=mesh, in_specs=placed, out_specs=P("tmpl", ("parts", "chan")), check_vma=False
    )
```

```python
import functools

import jax
import jax.numpy as jnp
from jax import lax
from jax.experimental import pallas as pl
from jax.experimental.pallas import tpu as pltpu
from jax.sharding import PartitionSpec as P

SPAN = 256
BLK = 256
LANE = 128
MESH = pl.DeviceIdType.MESH
PIECES = 2


def left(x, count):
    size = x.shape[-1]
    count = count % size
    return x if count == 0 else pltpu.roll(x, size - count, x.ndim - 1)


def kernel(
    ntm, nch, lend, raw_hbm, taps_ref, tmpl_hbm, mask_hbm, offs_ref, out_ref,
    raw, tap_row, tmpl, mask, skewed, shaped, rall, prod, qacc, units, num_out, en_out,
    num_in, en_in, guest, gacc, gsum, load_sem, raw_sem, recv_sem, right_sem, left_sem,
    unit_right, unit_left, unit_recv, num_send, num_recv, en_send, en_recv, guest_sem, gsum_sem,
):
    z = lax.axis_index("tmpl")
    c = lax.axis_index("chan")
    rows = raw.shape[0]
    group, tlen, local = tmpl.shape
    nblk = rall.shape[0]
    total = nblk * BLK
    unit = min(LANE, rows)
    nun = rows // unit

    def load_raw(n, first):
        at = pl.ds(0, BLK + LANE) if first else pl.ds(pl.multiple_of(n * BLK + LANE, LANE), BLK)
        return pltpu.make_async_copy(raw_hbm.at[:, at], raw.at[:, at], raw_sem.at[n])

    for n in range(nblk):
        load_raw(n, n == 0).start()
    loads = [
        pltpu.make_async_copy(tmpl_hbm, tmpl, load_sem.at[0]),
        pltpu.make_async_copy(
            mask_hbm.at[:, pl.ds(pl.multiple_of(c * local, LANE), local)], mask, load_sem.at[1]
        ),
    ]
    for item in loads:
        item.start()

    barrier = pltpu.get_barrier_semaphore()
    @pl.when(z < ntm - 1)
    def _():
        pl.semaphore_signal(
            barrier, inc=1, device_id={"tmpl": lax.rem(z + 1, ntm)}, device_id_type=MESH
        )

    @pl.when(z > 0)
    def _():
        pl.semaphore_signal(
            barrier, inc=1, device_id={"tmpl": lax.rem(z - 1 + ntm, ntm)}, device_id_type=MESH
        )

    for d in range(1, nch):
        pl.semaphore_signal(
            barrier, inc=1, device_id={"chan": lax.rem(c + d, nch)}, device_id_type=MESH
        )

    tap_row[...] = jnp.zeros_like(tap_row)
    tap_row[:, : taps_ref.shape[1]] = taps_ref[...]
    band = pltpu.roll(
        jnp.broadcast_to(tap_row[...], (LANE, 2 * LANE)), 0, 1, stride=1, stride_axis=0
    )
    band_hi = band.astype(jnp.bfloat16)
    band_lo = (band - band_hi.astype(jnp.float32)).astype(jnp.bfloat16)
    qacc[...] = jnp.zeros_like(qacc)
    is_end = (z == 0) | (z == ntm - 1)
    is_helper = (z == 1) | (z == ntm - 2)
    inward = jnp.where(z == 0, 1, ntm - 2)
    outward = jnp.where(z == 1, 0, ntm - 1)
    if lend:
        @pl.when(is_end)
        def _():
            at = pl.ds(pl.multiple_of(inward * rows, rows), rows)
            for n in range(nblk):
                rall[n, at, :] = jnp.zeros((rows, BLK), jnp.bfloat16)

    load_raw(0, True).wait()
    pl.semaphore_wait(
        barrier, jnp.where(z < ntm - 1, 1, 0) + jnp.where(z > 0, 1, 0) + (nch - 1)
    )

    def chunk(src, n):
        return rall.at[n, pl.ds(pl.multiple_of(src * rows, rows), rows), :]

    def hop(src, n, h, sems, step):
        height = rows // PIECES
        at = pl.ds(pl.multiple_of(src * rows + h * height, height), height)
        return pltpu.make_async_remote_copy(
            src_ref=rall.at[n, at, :],
            dst_ref=rall.at[n, at, :],
            send_sem=sems.at[src, n * PIECES + h],
            recv_sem=recv_sem.at[src, n * PIECES + h],
            device_id={"tmpl": lax.rem(z + step + ntm, ntm)},
            device_id_type=MESH,
        )

    def contract(a, b):
        return lax.dot_general(
            a, b, (((1,), (1,)), ((), ())), preferred_element_type=jnp.float32
        )

    def fir(n, carry):
        x = raw[:, pl.ds(pl.multiple_of(n * BLK, BLK), BLK + LANE)]
        hi = x.astype(jnp.bfloat16)
        lo = (x - hi.astype(jnp.float32)).astype(jnp.bfloat16)
        for half in range(BLK // LANE):
            a = hi[:, half * LANE : half * LANE + 2 * LANE]
            b = lo[:, half * LANE : half * LANE + 2 * LANE]
            y = contract(a, band_hi) + (contract(b, band_hi) + contract(a, band_lo))
            y = y.astype(jnp.bfloat16)
            rall[
                n, pl.ds(pl.multiple_of(z * rows, rows), rows), half * LANE : half * LANE + LANE
            ] = y
            y = y.astype(jnp.float32)
            y = y * y
            at = pl.ds(pl.multiple_of(n * BLK + half * LANE, LANE), LANE)
            for u in range(nun):
                units[z, u : u + 1, at] = jnp.sum(
                    y[u * unit : (u + 1) * unit], axis=0, keepdims=True
                )

        return carry

    def send_own(n, carry):
        @pl.when(z < ntm - 1 - lend)
        def _():
            for h in range(PIECES):
                hop(z, n, h, right_sem, 1).start()

        @pl.when(z > lend)
        def _():
            for h in range(PIECES):
                hop(z, n, h, left_sem, -1).start()

        return carry

    def fir_next(n, carry):
        load_raw(n, False).wait()
        return fir(n, carry)

    def unit_hop(src, sems, step):
        return pltpu.make_async_remote_copy(
            src_ref=units.at[src],
            dst_ref=units.at[src],
            send_sem=sems.at[src],
            recv_sem=unit_recv.at[src],
            device_id={"tmpl": lax.rem(z + step + ntm, ntm)},
            device_id_type=MESH,
        )

    fir(0, 0)
    send_own(0, 0)
    lax.fori_loop(1, nblk, fir_next, 0)

    @pl.when(z < ntm - 1)
    def _():
        unit_hop(z, unit_right, 1).start()

    @pl.when(z > 0)
    def _():
        unit_hop(z, unit_left, -1).start()

    lax.fori_loop(1, nblk, send_own, 0)

    loads[0].wait()
    loads[1].wait()

    def shape_cols(i, carry):
        cols = pl.ds(pl.multiple_of(i * LANE, LANE), LANE)
        flags = mask[:, cols].astype(jnp.float32)
        for k in range(group):
            v = tmpl[k, :, cols].astype(jnp.float32)
            power = jnp.mean(v * v, axis=0, keepdims=True)
            scale = flags[k : k + 1, :] / jnp.sqrt(power + 1e-06)
            skewed[pl.ds(k, tlen, stride=group), :] = v * scale
        shaped[:, cols] = skewed[...].astype(jnp.bfloat16)
        return carry

    lax.fori_loop(0, local // LANE, shape_cols, 0)

    def lend_copy(peer):
        cols = pl.ds(pl.multiple_of(inward * rows, rows), rows)
        return pltpu.make_async_remote_copy(
            src_ref=shaped.at[:, cols],
            dst_ref=guest,
            send_sem=guest_sem.at[0],
            recv_sem=guest_sem.at[1],
            device_id={"tmpl": peer},
            device_id_type=MESH,
        )

    def gsum_copy(peer):
        return pltpu.make_async_remote_copy(
            src_ref=gacc.at[:, pl.ds(BLK, total)],
            dst_ref=gsum,
            send_sem=gsum_sem.at[0],
            recv_sem=gsum_sem.at[1],
            device_id={"tmpl": peer},
            device_id_type=MESH,
        )

    if lend:
        @pl.when(is_end)
        def _():
            lend_copy(inward).start()

    offs = jnp.zeros((group, 1), jnp.int32)
    index = lax.broadcasted_iota(jnp.int32, (group, 1), 0)
    for k in range(group):
        offs = jnp.where(index == k, offs_ref[k], offs)

    def shift_rows(x):
        amount = jnp.broadcast_to(offs, x.shape)
        bit = 1
        while bit < SPAN - tlen + 1:
            x = jnp.where((amount & bit) != 0, left(x, bit), x)
            bit *= 2
        return x

    def spread(x, own_ref, in_ref, send, recv):
        lag = own_ref.shape[2]
        for j in range(nch):
            own_ref[j] = x[:, j * lag : (j + 1) * lag]
        for d in range(1, nch):
            other = lax.rem(c + d, nch)
            pltpu.make_async_remote_copy(
                src_ref=own_ref.at[other],
                dst_ref=in_ref.at[d],
                send_sem=send.at[d],
                recv_sem=recv.at[d],
                device_id={"chan": other},
                device_id_type=MESH,
            ).start()

    def collect(own_ref, in_ref, send, recv):
        value = own_ref[c]
        for d in range(1, nch):
            pltpu.make_async_remote_copy(
                src_ref=own_ref.at[lax.rem(c + d, nch)],
                dst_ref=in_ref.at[d],
                send_sem=send.at[d],
                recv_sem=recv.at[d],
                device_id={"chan": lax.rem(c + d, nch)},
                device_id_type=MESH,
            ).wait()
            value = value + in_ref[d]
        return value

    def unit_arrive(d):
        @pl.when(z - d >= 0)
        def _():
            src = lax.rem(z - d + ntm, ntm)
            unit_hop(src, unit_right, 1).wait_recv()

            @pl.when(z < ntm - 1)
            def _():
                unit_hop(src, unit_right, 1).start()

        @pl.when(z + d < ntm)
        def _():
            src = lax.rem(z + d, ntm)
            unit_hop(src, unit_left, -1).wait_recv()

            @pl.when(z > 0)
            def _():
                unit_hop(src, unit_left, -1).start()

    def send_energy():
        masses = jnp.zeros((group, total), jnp.float32)
        for s in range(ntm):
            for u in range(nun):
                at = s * rows + u * unit
                flag = mask[:, at : at + 1].astype(jnp.float32)
                masses = masses + flag * units[s, u : u + 1, :]
        window, width, place, energy = masses, 1, 0, None
        while width <= tlen:
            if tlen & width:
                piece = left(window, place)
                energy = piece if energy is None else energy + piece
                place += width
            window = window + left(window, width)
            width *= 2
        spread(shift_rows(energy), en_out, en_in, en_send, en_recv)

    def arrive(d, n):
        near = lend if d == 1 else 0

        @pl.when((z - d >= 0) & (z < ntm - near))
        def _():
            src = lax.rem(z - d + ntm, ntm)
            for h in range(PIECES):
                hop(src, n, h, right_sem, 1).wait_recv()

                @pl.when(z < ntm - 1)
                def _():
                    hop(src, n, h, right_sem, 1).start()

        @pl.when((z + d < ntm) & (z >= near))
        def _():
            src = lax.rem(z + d, ntm)
            for h in range(PIECES):
                hop(src, n, h, left_sem, -1).wait_recv()

                @pl.when(z > 0)
                def _():
                    hop(src, n, h, left_sem, -1).start()

    def skew(n, weights, samples, acc):
        prod[...] = jnp.dot(weights, samples, preferred_element_type=jnp.float32)
        blank = jnp.zeros((group, LANE), jnp.float32)
        total_acc = jnp.zeros((group, 2 * BLK), jnp.float32)
        for g in range(min(LANE, tlen)):
            low = prod[group * g : group * (g + 1), :]
            first, second = low[:, :LANE], low[:, LANE:]
            carry_in = blank
            if g + LANE < tlen:
                high = prod[group * (g + LANE) : group * (g + LANE + 1), :]
                carry_in = high[:, :LANE]
                first = first + high[:, LANE:]
            wide = jnp.concatenate([blank, carry_in, first, second], axis=1)
            total_acc = total_acc + left(wide, g)
        at = pl.ds(pl.multiple_of(n * BLK, BLK), 2 * BLK)
        acc[:, at] = acc[:, at] + total_acc

    def block(n, carry):
        for d in range(max(1, ntm // 2), ntm):
            arrive(d, n)

        @pl.when(n == min(1, nblk - 1))
        def _():
            for d in range(max(1, ntm // 2), ntm):
                unit_arrive(d)
            send_energy()

        skew(n, shaped[...], rall[n], qacc)
        return carry

    def guest_block(n, carry):
        skew(n, guest[...], chunk(z, n)[...], gacc)
        return carry

    def step(d):
        def body(n, carry):
            arrive(d, n)

            @pl.when(n == 0)
            def _():
                unit_arrive(d)

            return carry

        lax.fori_loop(0, nblk, body, 0)

    for d in range(1, max(1, ntm // 2)):
        step(d)
    lax.fori_loop(0, nblk, block, 0)

    if lend:
        @pl.when(is_helper)
        def _():
            gacc[...] = jnp.zeros_like(gacc)
            lend_copy(outward).wait_recv()
            lax.fori_loop(0, nblk, guest_block, 0)
            gsum_copy(outward).start()

        @pl.when(is_end)
        def _():
            gsum_copy(inward).wait_recv()
            qacc[:, BLK:] = qacc[:, BLK:] + gsum[...]

    spread(shift_rows(qacc[:, BLK:]), num_out, num_in, num_send, num_recv)
    energy = collect(en_out, en_in, en_send, en_recv)
    numerator = collect(num_out, num_in, num_send, num_recv)
    out_ref[...] = numerator / jnp.sqrt(energy)

    def drain(n, carry):
        for s in range(ntm):
            @pl.when((s <= z) & (z < ntm - 1) & ((s != z) | (z < ntm - 1 - lend)))
            def _():
                for h in range(PIECES):
                    hop(s, n, h, right_sem, 1).wait_send()

            @pl.when((s >= z) & (z > 0) & ((s != z) | (z > lend)))
            def _():
                for h in range(PIECES):
                    hop(s, n, h, left_sem, -1).wait_send()

        return carry

    lax.fori_loop(0, nblk, drain, 0)
    for s in range(ntm):
        @pl.when((s <= z) & (z < ntm - 1))
        def _():
            unit_hop(s, unit_right, 1).wait_send()

        @pl.when((s >= z) & (z > 0))
        def _():
            unit_hop(s, unit_left, -1).wait_send()

    if lend:
        @pl.when(is_end)
        def _():
            lend_copy(inward).wait_send()

        @pl.when(is_helper)
        def _():
            gsum_copy(outward).wait_send()


def shards(raw_traces, filter_taps, templates, offsets, channel_mask):
    ntm = lax.axis_size("tmpl")
    nch = lax.axis_size("chan")
    rows, length = raw_traces.shape
    group, tlen, local = templates.shape
    nblk = (length - filter_taps.shape[0] + 1) // BLK
    total = nblk * BLK
    lag = (total - SPAN) // nch
    nun = rows // min(LANE, rows)
    lend = int(ntm >= 4 and rows % LANE == 0)
    f32, bf16, dma = jnp.float32, jnp.bfloat16, pltpu.SemaphoreType.DMA
    any_spec = pl.BlockSpec(memory_space=pl.ANY)
    vmem_spec = pl.BlockSpec(memory_space=pltpu.VMEM)
    return pl.pallas_call(
        functools.partial(kernel, ntm, nch, lend),
        out_shape=jax.ShapeDtypeStruct((group, lag), f32),
        in_specs=[
            any_spec, vmem_spec, any_spec, any_spec, pl.BlockSpec(memory_space=pltpu.SMEM),
        ],
        out_specs=vmem_spec,
        scratch_shapes=[
            pltpu.VMEM((rows, length), f32),
            pltpu.VMEM((1, 2 * LANE), f32),
            pltpu.VMEM((group, tlen, local), bf16),
            pltpu.VMEM((group, local), jnp.int32),
            pltpu.VMEM((group * tlen, LANE), f32),
            pltpu.VMEM((group * tlen, local), bf16),
            pltpu.VMEM((nblk, local, BLK), bf16),
            pltpu.VMEM((group * tlen, BLK), f32),
            pltpu.VMEM((group, BLK + total), f32),
            pltpu.VMEM((ntm, nun, total), f32),
            pltpu.VMEM((nch, group, lag), f32),
            pltpu.VMEM((nch, group, lag), f32),
            pltpu.VMEM((nch, group, lag), f32),
            pltpu.VMEM((nch, group, lag), f32),
            pltpu.VMEM((group * tlen, rows if lend else LANE), bf16),
            pltpu.VMEM((group, BLK + total), f32),
            pltpu.VMEM((group, total), f32),
            dma((2,)),
            dma((nblk,)),
            dma((ntm, nblk * PIECES)),
            dma((ntm, nblk * PIECES)),
            dma((ntm, nblk * PIECES)),
            dma((ntm,)),
            dma((ntm,)),
            dma((ntm,)),
            dma((nch,)),
            dma((nch,)),
            dma((nch,)),
            dma((nch,)),
            dma((2,)),
            dma((2,)),
        ],
        compiler_params=pltpu.CompilerParams(
            collective_id=0, has_side_effects=True, vmem_limit_bytes=60 * 1024 * 1024
        ),
    )(raw_traces, filter_taps.reshape(1, -1), templates, channel_mask, offsets)


def solution(mesh):
    placed = (
        P(("chan", "tmpl"), "parts"),
        P(),
        P("tmpl", None, "chan"),
        P("tmpl"),
        P("tmpl", None),
    )
    return jax.shard_map(
        shards, mesh=mesh, in_specs=placed, out_specs=P("tmpl", ("parts", "chan")), check_vma=False
    )
```

```python
import functools

import jax
import jax.numpy as jnp
from jax import lax
from jax.experimental import pallas as pl
from jax.experimental.pallas import tpu as pltpu
from jax.sharding import PartitionSpec as P

SPAN = 256
BLK = 256
LANE = 128
MESH = pl.DeviceIdType.MESH
PIECES = 1


def left(x, count):
    size = x.shape[-1]
    count = count % size
    return x if count == 0 else pltpu.roll(x, size - count, x.ndim - 1)


def kernel(
    ntm, nch, lend, raw_hbm, taps_hbm, tmpl_hbm, mask_hbm, offs_hbm, out_ref,
    taps_ref, offs_ref, raw, tap_row, tmpl, mask, skewed, shaped, rall, prod, qacc, units, num_out, en_out,
    num_in, en_in, guest, gacc, gsum, load_sem, raw_sem, recv_sem, right_sem, left_sem,
    unit_right, unit_left, unit_recv, num_send, num_recv, en_send, en_recv, guest_sem, gsum_sem,
):
    z = lax.axis_index("tmpl")
    c = lax.axis_index("chan")
    rows = raw.shape[0]
    group, tlen, local = tmpl.shape
    nblk = rall.shape[0]
    total = nblk * BLK
    unit = min(LANE, rows)
    nun = rows // unit

    def load_raw(n, first):
        at = pl.ds(0, BLK + LANE) if first else pl.ds(pl.multiple_of(n * BLK + LANE, LANE), BLK)
        return pltpu.make_async_copy(raw_hbm.at[:, at], raw.at[:, at], raw_sem.at[n])

    load_taps = pltpu.make_async_copy(taps_hbm, taps_ref, load_sem.at[2])
    load_taps.start()
    for n in range(nblk):
        load_raw(n, n == 0).start()
    loads = [
        pltpu.make_async_copy(tmpl_hbm, tmpl, load_sem.at[0]),
        pltpu.make_async_copy(
            mask_hbm.at[:, pl.ds(pl.multiple_of(c * local, LANE), local)], mask, load_sem.at[1]
        ),
        pltpu.make_async_copy(offs_hbm, offs_ref, load_sem.at[3]),
    ]
    for item in loads:
        item.start()

    barrier = pltpu.get_barrier_semaphore()
    @pl.when(z < ntm - 1)
    def _():
        pl.semaphore_signal(
            barrier, inc=1, device_id={"tmpl": lax.rem(z + 1, ntm)}, device_id_type=MESH
        )

    @pl.when(z > 0)
    def _():
        pl.semaphore_signal(
            barrier, inc=1, device_id={"tmpl": lax.rem(z - 1 + ntm, ntm)}, device_id_type=MESH
        )

    for d in range(1, nch):
        pl.semaphore_signal(
            barrier, inc=1, device_id={"chan": lax.rem(c + d, nch)}, device_id_type=MESH
        )

    tap_row[...] = jnp.zeros_like(tap_row)
    load_taps.wait()
    tap_row[:, : taps_ref.shape[1]] = taps_ref[...]
    band = pltpu.roll(
        jnp.broadcast_to(tap_row[...], (LANE, 2 * LANE)), 0, 1, stride=1, stride_axis=0
    )
    band_hi = band.astype(jnp.bfloat16)
    band_lo = (band - band_hi.astype(jnp.float32)).astype(jnp.bfloat16)
    qacc[...] = jnp.zeros_like(qacc)
    is_end = (z == 0) | (z == ntm - 1)
    is_helper = (z == 1) | (z == ntm - 2)
    inward = jnp.where(z == 0, 1, ntm - 2)
    outward = jnp.where(z == 1, 0, ntm - 1)
    if lend:
        @pl.when(is_end)
        def _():
            at = pl.ds(pl.multiple_of(inward * rows, rows), rows)
            for n in range(nblk):
                rall[n, at, :] = jnp.zeros((rows, BLK), jnp.bfloat16)

    load_raw(0, True).wait()

    def chunk(src, n):
        return rall.at[n, pl.ds(pl.multiple_of(src * rows, rows), rows), :]

    def hop(src, n, h, sems, step):
        height = rows // PIECES
        at = pl.ds(pl.multiple_of(src * rows + h * height, height), height)
        return pltpu.make_async_remote_copy(
            src_ref=rall.at[n, at, :],
            dst_ref=rall.at[n, at, :],
            send_sem=sems.at[src, n * PIECES + h],
            recv_sem=recv_sem.at[src, n * PIECES + h],
            device_id={"tmpl": lax.rem(z + step + ntm, ntm)},
            device_id_type=MESH,
        )

    def contract(a, b):
        return lax.dot_general(
            a, b, (((1,), (1,)), ((), ())), preferred_element_type=jnp.float32
        )

    def fir(n, carry):
        x = raw[:, pl.ds(pl.multiple_of(n * BLK, BLK), BLK + LANE)]
        hi = x.astype(jnp.bfloat16)
        lo = (x - hi.astype(jnp.float32)).astype(jnp.bfloat16)
        for half in range(BLK // LANE):
            a = hi[:, half * LANE : half * LANE + 2 * LANE]
            b = lo[:, half * LANE : half * LANE + 2 * LANE]
            y = contract(a, band_hi) + (contract(b, band_hi) + contract(a, band_lo))
            y = y.astype(jnp.bfloat16)
            rall[
                n, pl.ds(pl.multiple_of(z * rows, rows), rows), half * LANE : half * LANE + LANE
            ] = y
            y = y.astype(jnp.float32)
            y = y * y
            at = pl.ds(pl.multiple_of(n * BLK + half * LANE, LANE), LANE)
            for u in range(nun):
                units[z, u : u + 1, at] = jnp.sum(
                    y[u * unit : (u + 1) * unit], axis=0, keepdims=True
                )

        return carry

    def send_own(n, carry):
        @pl.when(z < ntm - 1 - lend)
        def _():
            for h in range(PIECES):
                hop(z, n, h, right_sem, 1).start()

        @pl.when(z > lend)
        def _():
            for h in range(PIECES):
                hop(z, n, h, left_sem, -1).start()

        return carry

    def fir_next(n, carry):
        load_raw(n, False).wait()
        return fir(n, carry)

    def unit_hop(src, sems, step):
        return pltpu.make_async_remote_copy(
            src_ref=units.at[src],
            dst_ref=units.at[src],
            send_sem=sems.at[src],
            recv_sem=unit_recv.at[src],
            device_id={"tmpl": lax.rem(z + step + ntm, ntm)},
            device_id_type=MESH,
        )

    fir(0, 0)
    pl.semaphore_wait(
        barrier, jnp.where(z < ntm - 1, 1, 0) + jnp.where(z > 0, 1, 0) + (nch - 1)
    )
    send_own(0, 0)
    lax.fori_loop(1, nblk, fir_next, 0)

    @pl.when(z < ntm - 1)
    def _():
        unit_hop(z, unit_right, 1).start()

    @pl.when(z > 0)
    def _():
        unit_hop(z, unit_left, -1).start()

    lax.fori_loop(1, nblk, send_own, 0)

    for item in loads:
        item.wait()

    def shape_cols(i, carry):
        cols = pl.ds(pl.multiple_of(i * LANE, LANE), LANE)
        flags = mask[:, cols].astype(jnp.float32)
        for k in range(group):
            v = tmpl[k, :, cols].astype(jnp.float32)
            power = jnp.mean(v * v, axis=0, keepdims=True)
            scale = flags[k : k + 1, :] / jnp.sqrt(power + 1e-06)
            skewed[pl.ds(k, tlen, stride=group), :] = v * scale
        shaped[:, cols] = skewed[...].astype(jnp.bfloat16)
        return carry

    lax.fori_loop(0, local // LANE, shape_cols, 0)

    cut = min(LANE, tlen) * group
    parts = [(0, cut), (cut, tlen * group - cut)]

    def lend_copy(p, peer):
        cols = pl.ds(pl.multiple_of(inward * rows, rows), rows)
        lines = pl.ds(*parts[p])
        return pltpu.make_async_remote_copy(
            src_ref=shaped.at[lines, cols],
            dst_ref=guest.at[lines, :],
            send_sem=guest_sem.at[0, p],
            recv_sem=guest_sem.at[1, p],
            device_id={"tmpl": peer},
            device_id_type=MESH,
        )

    def gsum_copy(peer):
        return pltpu.make_async_remote_copy(
            src_ref=gacc.at[:, pl.ds(BLK, total)],
            dst_ref=gsum,
            send_sem=gsum_sem.at[0],
            recv_sem=gsum_sem.at[1],
            device_id={"tmpl": peer},
            device_id_type=MESH,
        )

    if lend:
        @pl.when(is_end)
        def _():
            lend_copy(0, inward).start()
            lend_copy(1, inward).start()

    offs = jnp.zeros((group, 1), jnp.int32)
    index = lax.broadcasted_iota(jnp.int32, (group, 1), 0)
    for k in range(group):
        offs = jnp.where(index == k, offs_ref[k], offs)

    def shift_rows(x):
        amount = jnp.broadcast_to(offs, x.shape)
        bit = 1
        while bit < SPAN - tlen + 1:
            x = jnp.where((amount & bit) != 0, left(x, bit), x)
            bit *= 2
        return x

    def spread(x, own_ref, in_ref, send, recv):
        lag = own_ref.shape[2]
        for j in range(nch):
            own_ref[j] = x[:, j * lag : (j + 1) * lag]
        for d in range(1, nch):
            other = lax.rem(c + d, nch)
            pltpu.make_async_remote_copy(
                src_ref=own_ref.at[other],
                dst_ref=in_ref.at[d],
                send_sem=send.at[d],
                recv_sem=recv.at[d],
                device_id={"chan": other},
                device_id_type=MESH,
            ).start()

    def collect(own_ref, in_ref, send, recv):
        value = own_ref[c]
        for d in range(1, nch):
            pltpu.make_async_remote_copy(
                src_ref=own_ref.at[lax.rem(c + d, nch)],
                dst_ref=in_ref.at[d],
                send_sem=send.at[d],
                recv_sem=recv.at[d],
                device_id={"chan": lax.rem(c + d, nch)},
                device_id_type=MESH,
            ).wait()
            value = value + in_ref[d]
        return value

    def unit_arrive(d):
        @pl.when(z - d >= 0)
        def _():
            src = lax.rem(z - d + ntm, ntm)
            unit_hop(src, unit_right, 1).wait_recv()

            @pl.when(z < ntm - 1)
            def _():
                unit_hop(src, unit_right, 1).start()

        @pl.when(z + d < ntm)
        def _():
            src = lax.rem(z + d, ntm)
            unit_hop(src, unit_left, -1).wait_recv()

            @pl.when(z > 0)
            def _():
                unit_hop(src, unit_left, -1).start()

    def send_energy():
        masses = jnp.zeros((group, total), jnp.float32)
        for s in range(ntm):
            for u in range(nun):
                at = s * rows + u * unit
                flag = mask[:, at : at + 1].astype(jnp.float32)
                masses = masses + flag * units[s, u : u + 1, :]
        window, width, place, energy = masses, 1, 0, None
        while width <= tlen:
            if tlen & width:
                piece = left(window, place)
                energy = piece if energy is None else energy + piece
                place += width
            window = window + left(window, width)
            width *= 2
        spread(shift_rows(energy), en_out, en_in, en_send, en_recv)

    def arrive(d, n):
        near = lend if d == 1 else 0

        @pl.when((z - d >= 0) & (z < ntm - near))
        def _():
            src = lax.rem(z - d + ntm, ntm)
            for h in range(PIECES):
                hop(src, n, h, right_sem, 1).wait_recv()

                @pl.when(z < ntm - 1)
                def _():
                    hop(src, n, h, right_sem, 1).start()

        @pl.when((z + d < ntm) & (z >= near))
        def _():
            src = lax.rem(z + d, ntm)
            for h in range(PIECES):
                hop(src, n, h, left_sem, -1).wait_recv()

                @pl.when(z > 0)
                def _():
                    hop(src, n, h, left_sem, -1).start()

    def skew(n, weights, samples, acc, begin, end):
        prod[: weights.shape[0], :] = jnp.dot(
            weights, samples, preferred_element_type=jnp.float32
        )
        blank = jnp.zeros((group, LANE), jnp.float32)
        total_acc = jnp.zeros((group, 2 * BLK), jnp.float32)

        def row(tap):
            if tap < begin or tap >= end:
                return None
            line = (tap - begin) * group
            return prod[line : line + group, :]

        for g in range(min(LANE, tlen)):
            low, high = row(g), row(g + LANE)
            if low is None and high is None:
                continue
            carry_in, first, second = blank, blank, blank
            if low is not None:
                first, second = low[:, :LANE], low[:, LANE:]
            if high is not None:
                carry_in = high[:, :LANE]
                first = high[:, LANE:] if low is None else first + high[:, LANE:]
            wide = jnp.concatenate([blank, carry_in, first, second], axis=1)
            total_acc = total_acc + left(wide, g)
        at = pl.ds(pl.multiple_of(n * BLK, BLK), 2 * BLK)
        acc[:, at] = acc[:, at] + total_acc

    def guest_block(p, n, carry):
        line, count = parts[p]
        weights = guest[line : line + count, :]
        skew(n, weights, chunk(z, n)[...], gacc, line // group, (line + count) // group)
        return carry

    def block(n, carry):
        for d in range(max(1, ntm // 2), ntm):
            arrive(d, n)

        @pl.when(n == min(1, nblk - 1))
        def _():
            for d in range(max(1, ntm // 2), ntm):
                unit_arrive(d)
            send_energy()

        if lend:
            @pl.when((n == nblk - 1) & is_helper)
            def _():
                gacc[...] = jnp.zeros_like(gacc)
                lend_copy(0, outward).wait_recv()
                lax.fori_loop(0, nblk, functools.partial(guest_block, 0), 0)

        skew(n, shaped[...], rall[n], qacc, 0, tlen)
        return carry

    def step(d):
        def body(n, carry):
            arrive(d, n)

            @pl.when(n == 0)
            def _():
                unit_arrive(d)

            return carry

        lax.fori_loop(0, nblk, body, 0)

    for d in range(1, max(1, ntm // 2)):
        step(d)
    lax.fori_loop(0, nblk, block, 0)

    if lend:
        @pl.when(is_helper)
        def _():
            lend_copy(1, outward).wait_recv()
            lax.fori_loop(0, nblk, functools.partial(guest_block, 1), 0)
            gsum_copy(outward).start()

        @pl.when(is_end)
        def _():
            gsum_copy(inward).wait_recv()
            qacc[:, BLK:] = qacc[:, BLK:] + gsum[...]

    spread(shift_rows(qacc[:, BLK:]), num_out, num_in, num_send, num_recv)
    energy = collect(en_out, en_in, en_send, en_recv)
    numerator = collect(num_out, num_in, num_send, num_recv)
    out_ref[...] = numerator / jnp.sqrt(energy)

    def drain(n, carry):
        for s in range(ntm):
            @pl.when((s <= z) & (z < ntm - 1) & ((s != z) | (z < ntm - 1 - lend)))
            def _():
                for h in range(PIECES):
                    hop(s, n, h, right_sem, 1).wait_send()

            @pl.when((s >= z) & (z > 0) & ((s != z) | (z > lend)))
            def _():
                for h in range(PIECES):
                    hop(s, n, h, left_sem, -1).wait_send()

        return carry

    lax.fori_loop(0, nblk, drain, 0)
    for s in range(ntm):
        @pl.when((s <= z) & (z < ntm - 1))
        def _():
            unit_hop(s, unit_right, 1).wait_send()

        @pl.when((s >= z) & (z > 0))
        def _():
            unit_hop(s, unit_left, -1).wait_send()

    if lend:
        @pl.when(is_end)
        def _():
            lend_copy(0, inward).wait_send()
            lend_copy(1, inward).wait_send()

        @pl.when(is_helper)
        def _():
            gsum_copy(outward).wait_send()


def shards(raw_traces, filter_taps, templates, offsets, channel_mask):
    ntm = lax.axis_size("tmpl")
    nch = lax.axis_size("chan")
    rows, length = raw_traces.shape
    group, tlen, local = templates.shape
    nblk = (length - filter_taps.shape[0] + 1) // BLK
    total = nblk * BLK
    lag = (total - SPAN) // nch
    nun = rows // min(LANE, rows)
    lend = int(ntm >= 4 and rows % LANE == 0 and tlen > LANE)
    f32, bf16, dma = jnp.float32, jnp.bfloat16, pltpu.SemaphoreType.DMA
    any_spec = pl.BlockSpec(memory_space=pl.ANY)
    vmem_spec = pl.BlockSpec(memory_space=pltpu.VMEM)
    return pl.pallas_call(
        functools.partial(kernel, ntm, nch, lend),
        out_shape=jax.ShapeDtypeStruct((group, lag), f32),
        in_specs=[
            any_spec, any_spec, any_spec, any_spec, any_spec,
        ],
        out_specs=vmem_spec,
        scratch_shapes=[
            pltpu.VMEM((1, filter_taps.shape[0]), f32),
            pltpu.SMEM((group,), jnp.int32),
            pltpu.VMEM((rows, length), f32),
            pltpu.VMEM((1, 2 * LANE), f32),
            pltpu.VMEM((group, tlen, local), bf16),
            pltpu.VMEM((group, local), jnp.int32),
            pltpu.VMEM((group * tlen, LANE), f32),
            pltpu.VMEM((group * tlen, local), bf16),
            pltpu.VMEM((nblk, local, BLK), bf16),
            pltpu.VMEM((group * tlen, BLK), f32),
            pltpu.VMEM((group, BLK + total), f32),
            pltpu.VMEM((ntm, nun, total), f32),
            pltpu.VMEM((nch, group, lag), f32),
            pltpu.VMEM((nch, group, lag), f32),
            pltpu.VMEM((nch, group, lag), f32),
            pltpu.VMEM((nch, group, lag), f32),
            pltpu.VMEM((group * tlen, rows if lend else LANE), bf16),
            pltpu.VMEM((group, BLK + total), f32),
            pltpu.VMEM((group, total), f32),
            dma((4,)),
            dma((nblk,)),
            dma((ntm, nblk * PIECES)),
            dma((ntm, nblk * PIECES)),
            dma((ntm, nblk * PIECES)),
            dma((ntm,)),
            dma((ntm,)),
            dma((ntm,)),
            dma((nch,)),
            dma((nch,)),
            dma((nch,)),
            dma((nch,)),
            dma((2, 2)),
            dma((2,)),
        ],
        compiler_params=pltpu.CompilerParams(
            collective_id=0, has_side_effects=True, vmem_limit_bytes=60 * 1024 * 1024
        ),
    )(raw_traces, filter_taps.reshape(1, -1), templates, channel_mask, offsets)


def solution(mesh):
    placed = (
        P(("chan", "tmpl"), "parts"),
        P(),
        P("tmpl", None, "chan"),
        P("tmpl"),
        P("tmpl", None),
    )
    return jax.shard_map(
        shards, mesh=mesh, in_specs=placed, out_specs=P("tmpl", ("parts", "chan")), check_vma=False
    )
```
